32 devices in a mesh: dp: 16 (over z, y, core), grp: 2 (over x).
Axes of the slice: x: 2, y: 2, z: 4, core: 2. Of those that a mesh axis runs over, the one named last changes fastest.
Arguments:
- key_inputs: bfloat16 [4096, 4096], P(('dp', 'grp'))
- query_inputs: bfloat16 [4096, 4096], P(('dp', 'grp'))
- key_weight: bfloat16 [4096, 256], replicated
- query_weight: bfloat16 [4096, 256], replicated
- queue: bfloat16 [4096, 256], P('grp')
- shuffle_masks: int32 [8], replicated, may hold values from 1 to 15, as said below
- write_pointer: int32 [1], replicated, may hold values from 0 to 4095
- positives: int32 [4096], P(('dp', 'grp')), may hold values from 0 to 255
Outputs:
- losses: float32 [4096], P(('dp', 'grp'))
- mean_loss: float32 [1], replicated
The draws below stay inside these ranges and needn't reach their ends.
Inputs may be any that keep to these rules, and one draw needn't show every extreme that they name: `shuffle_masks`: every entry lies in 1 to 16 - 1, so no data index is matched with itself; both ends occur in every draw.
All inputs are finite; a program needn't handle non-finite values.
Results may differ from the reference program's by a relative error of at most 0.00041.
Values may be sent and summed in bfloat16 or wider, within the bound.
A program may use at most 64 MiB of HBM per device.

```python
import math
import jax
import jax.numpy as jnp
from jax import lax

D_IN = 4096
PROJ = 256
B_DEV = 128
SUBS = 8
QUEUE = 4096
SUB = 16
GKEYS = 256
BATCH = 4096
N_DP = 16
N_GRP = 2


cluster_count = 32


def draw_shuffle_masks(key, part):
    values = jax.random.randint(jax.random.fold_in(key, 11), (SUBS,), 1, N_DP, dtype=jnp.int32)
    where_top = jax.random.randint(jax.random.fold_in(key, 12), (), 0, SUBS, dtype=jnp.int32)
    values = values.at[where_top].set(N_DP - 1)
    values = values.at[jnp.mod(where_top + 1, SUBS)].set(1)
    return values.astype(jnp.int32)


def skewed_clusters(key, salt, count):
    pick_one = jax.random.randint(jax.random.fold_in(key, salt), (count,), 0, cluster_count, dtype=jnp.int32)
    pick_two = jax.random.randint(jax.random.fold_in(key, salt + 1), (count,), 0, cluster_count, dtype=jnp.int32)
    return jnp.minimum(pick_one, pick_two)


def positive_slots(key):
    return jax.random.randint(jax.random.fold_in(key, 61), (BATCH,), 0, GKEYS, dtype=jnp.int32)


def image_rows(key, row_ids):
    clusters = skewed_clusters(key, 21, BATCH)[row_ids]
    cluster_lift = 2.0 * math.sqrt(D_IN)
    columns = jnp.arange(D_IN, dtype=jnp.int32)
    row_base = jax.random.fold_in(key, 51)

    def one_row(row_id, cluster):
        row_seed = jax.random.fold_in(row_base, row_id)
        jitter = jax.random.normal(row_seed, (D_IN,), jnp.float32)
        return jitter + cluster_lift * (columns == cluster).astype(jnp.float32)
    return jax.vmap(one_row)(row_ids, clusters)


def projection_weights(key):
    base_rows = jax.random.normal(jax.random.fold_in(key, 41), (D_IN, PROJ), jnp.float32)
    other_part = jax.random.normal(jax.random.fold_in(key, 42), (D_IN, PROJ), jnp.float32)
    weight_scale = 1.0 / math.sqrt(D_IN)
    key_matrix = base_rows * weight_scale
    query_matrix = (0.95 * base_rows + 0.3 * other_part) * weight_scale
    return (key_matrix, query_matrix)


def draw_positives(key, part):
    return positive_slots(key).astype(jnp.int32)


def draw_key_inputs(key, part):
    row_ids = jnp.arange(BATCH, dtype=jnp.int32)
    return image_rows(key, row_ids).astype(jnp.bfloat16)


def draw_query_inputs(key, part):
    image_ids = jnp.arange(BATCH, dtype=jnp.int32)
    row_ids = image_ids // GKEYS * GKEYS + positive_slots(key)
    base_rows = image_rows(key, row_ids)
    jitter = 0.5 * jax.random.normal(jax.random.fold_in(key, 62), (BATCH, D_IN), jnp.float32)
    return (base_rows + jitter).astype(jnp.bfloat16)


def draw_key_weight(key, part):
    return projection_weights(key)[0].astype(jnp.bfloat16)


def draw_query_weight(key, part):
    return projection_weights(key)[1].astype(jnp.bfloat16)


def draw_queue(key, part):
    key_matrix = projection_weights(key)[0]
    slot_clusters = skewed_clusters(key, 71, QUEUE)
    directions = key_matrix[slot_clusters] * math.sqrt(D_IN / PROJ)
    jitter = jax.random.normal(jax.random.fold_in(key, 73), (QUEUE, PROJ), jnp.float32)
    row_scale = jnp.exp(jax.random.uniform(jax.random.fold_in(key, 74), (QUEUE, 1), jnp.float32, math.log(0.7), math.log(1.4)))
    jitter = jitter / math.sqrt(PROJ)
    return (row_scale * (0.6 * directions + 0.8 * jitter)).astype(jnp.bfloat16)


def setup_inputs(seed: int = 0) -> dict:
    key_list = jax.random.split(jax.random.key(seed), 9)
    key_inputs = draw_key_inputs(jax.random.fold_in(key_list[8], 71), 0)
    query_inputs = draw_query_inputs(jax.random.fold_in(key_list[8], 71), 0)
    key_weight = draw_key_weight(jax.random.fold_in(key_list[8], 71), 0)
    query_weight = draw_query_weight(jax.random.fold_in(key_list[8], 71), 0)
    queue = draw_queue(jax.random.fold_in(key_list[8], 71), 0)
    shuffle_masks = draw_shuffle_masks(jax.random.fold_in(key_list[8], 71), 0)
    write_pointer = jax.random.randint(key_list[6], (1,), 0, QUEUE).astype(jnp.int32)
    positives = draw_positives(jax.random.fold_in(key_list[8], 71), 0)
    return {"key_inputs": key_inputs, "query_inputs": query_inputs, "key_weight": key_weight, "query_weight": query_weight, "queue": queue, "shuffle_masks": shuffle_masks, "write_pointer": write_pointer, "positives": positives}


epsilon = 1e-05
temper = 5.0

def reference(key_inputs, query_inputs, key_weight, query_weight, queue, shuffle_masks, write_pointer, positives):
    projected = jnp.dot(key_inputs, key_weight, preferred_element_type=jnp.float32)
    projected = projected.reshape(N_DP, N_GRP, SUBS, SUB, PROJ)
    data_ids = jnp.arange(N_DP, dtype=jnp.int32)
    partner = jnp.bitwise_xor(data_ids[:, None], shuffle_masks.astype(jnp.int32)[None, :])
    group_ids = jnp.arange(N_GRP, dtype=jnp.int32)
    sub_ids = jnp.arange(SUBS, dtype=jnp.int32)
    grouped = projected[partner[:, None, :], group_ids[None, :, None], sub_ids[None, None, :]]
    centre = lax.optimization_barrier(jnp.sum(grouped, axis=(2, 3))) / B_DEV
    second = lax.optimization_barrier(jnp.sum(grouped * grouped, axis=(2, 3))) / B_DEV
    spread = second - centre * centre
    row_centre = centre[partner[:, None, :], group_ids[None, :, None]][:, :, :, None, :]
    row_spread = spread[partner[:, None, :], group_ids[None, :, None]][:, :, :, None, :]
    normed = ((projected - row_centre) * lax.rsqrt(row_spread + epsilon)).reshape(BATCH, PROJ)
    keys = (normed * lax.rsqrt(lax.optimization_barrier(jnp.sum(normed * normed, axis=1, keepdims=True)) + 1e-06)).astype(jnp.bfloat16)
    raw_query = jnp.dot(query_inputs, query_weight, preferred_element_type=jnp.float32)
    queries = (raw_query * lax.rsqrt(lax.optimization_barrier(jnp.sum(raw_query * raw_query, axis=1, keepdims=True)) + 1e-06)).astype(jnp.bfloat16)
    slots = jnp.arange(QUEUE, dtype=jnp.int32)
    stale = jnp.mod(slots - write_pointer[0], QUEUE) < GKEYS

    def one_group(inputs):
        group_queries, group_keys, group_pos = inputs
        inner = temper * jnp.dot(group_queries, group_keys.T, preferred_element_type=jnp.float32)
        columns = jnp.arange(GKEYS, dtype=jnp.int32)
        pos_logit = lax.optimization_barrier(jnp.sum(jnp.where(columns[None, :] == group_pos[:, None], inner, 0.0), axis=1))
        scores = temper * jnp.dot(group_queries, queue.T, preferred_element_type=jnp.float32)
        queue_total = lax.optimization_barrier(jnp.sum(jnp.where(stale[None, :], 0.0, jnp.exp(scores)), axis=1))
        total = lax.optimization_barrier(jnp.sum(jnp.exp(inner), axis=1)) + queue_total
        return jnp.log(total) - pos_logit
    losses = lax.map(one_group, (queries.reshape(N_DP, GKEYS, PROJ), keys.reshape(N_DP, GKEYS, PROJ), positives.reshape(N_DP, GKEYS)))
    losses = losses.reshape(BATCH)
    mean_loss = (jnp.sum(losses) / BATCH).reshape(1)
    return (losses, mean_loss)
```

```python
import functools

import jax
import jax.numpy as jnp
from jax import lax
from jax.experimental import pallas as pl
from jax.experimental.pallas import tpu as pltpu
from jax.sharding import PartitionSpec as P

epsilon = 1e-05
temper = 5.0
MESH = pl.DeviceIdType.MESH
CHUNKS = 4
FIRST = 2


def each(count, body):
    def step(index, carry):
        body(index)
        return carry

    if count > 0:
        lax.fori_loop(0, count, step, 0, unroll=count if count <= 32 else 1)


def times_transposed(left, right):
    return lax.dot_general(
        left, right, (((1,), (1,)), ((), ())), preferred_element_type=jnp.float32
    )


def kernel(
    n_dp,
    n_grp,
    key_inputs,
    query_inputs,
    key_weight,
    query_weight,
    queue,
    shuffle_masks,
    write_pointer,
    positives,
    result,
    kx,
    kw,
    qx,
    qw,
    slots,
    projected,
    stats,
    means,
    scatters,
    group_queries,
    group_positives,
    queue_sums,
    totals,
    matches,
    masks_here,
    pointer_here,
    local_sem,
    stat_send,
    stat_recv,
    query_send,
    query_recv,
    pos_send,
    pos_recv,
    total_send,
    total_recv,
    match_send,
    match_recv,
    plane_sem,
):
    d_in, width = kw.shape
    rows = kx.shape[0]
    subs = means.shape[1]
    sub = rows // subs
    part = d_in // CHUNKS
    queue_rows = slots.shape[0]
    columns = n_grp * rows
    n_all = n_dp * n_grp
    me = lax.axis_index("dp")
    grp = lax.axis_index("grp")

    barrier = pltpu.get_barrier_semaphore()

    def greet(device):
        pl.semaphore_signal(barrier, inc=1, device_id=device, device_id_type=MESH)

    def group_member(k):
        return (me, lax.rem(grp + 1 + k, n_grp))

    loads = []
    for x_hbm, x, w_hbm, w in (
        (key_inputs, kx, key_weight, kw),
        (query_inputs, qx, query_weight, qw),
    ):
        for c in range(CHUNKS):
            span = pl.ds(c * part, part)
            loads.append((x_hbm.at[:, span], x.at[:, span]))
            loads.append((w_hbm.at[span, :], w.at[span, :]))
    loads.append((queue, slots))
    loads.append((positives, group_positives.at[grp]))
    loads.append((shuffle_masks, masks_here))
    loads.append((write_pointer, pointer_here))
    loads = [
        pltpu.make_async_copy(source, target, local_sem.at[index])
        for index, (source, target) in enumerate(loads)
    ]
    for load in loads[:FIRST]:
        load.start()
    queue_load, positives_load, masks_load, pointer_load = loads[-4:]
    each(n_dp - 1, lambda i: greet((me ^ (n_dp - 1 - i), grp)))
    each(n_grp - 1, lambda k: greet(group_member(k)))
    for load in loads[FIRST : 2 * CHUNKS]:
        load.start()

    def project(first, x, w, later):
        total = None
        for c in range(CHUNKS):
            loads[first + 2 * c].wait()
            loads[first + 2 * c + 1].wait()
            for load in later[c]:
                load.start()
            span = pl.ds(c * part, part)
            term = jnp.dot(x[:, span], w[span, :], preferred_element_type=jnp.float32)
            total = term if total is None else total + term
        return total

    after = [loads[2 * CHUNKS + 2 * c : 2 * CHUNKS + 2 * c + 2] for c in range(CHUNKS)]
    after[-1] = after[-1] + loads[4 * CHUNKS :]
    keys_raw = project(0, kx, kw, after)
    projected[...] = keys_raw
    blocks = keys_raw.reshape(subs, sub, width)
    centres = jnp.sum(blocks, axis=1) / sub
    apart = blocks - centres[:, None, :]
    base = centres[:1].astype(jnp.bfloat16)
    first_row = lax.broadcasted_iota(jnp.int32, (subs, width), 0) == 0
    coded = jnp.where(first_row, centres, centres - base.astype(jnp.float32))
    stats[me] = jnp.concatenate(
        [coded, jnp.sum(apart * apart, axis=1) / sub], axis=0
    ).astype(jnp.bfloat16)

    pl.semaphore_wait(barrier, n_dp + n_grp - 2)

    def remote(source, target, send, recv, device):
        return pltpu.make_async_remote_copy(
            src_ref=source,
            dst_ref=target,
            send_sem=send,
            recv_sem=recv,
            device_id=device,
            device_id_type=MESH,
        )

    neighbour = (me ^ 1, grp)

    def send_stats(i):
        j = n_dp - 2 - i
        device = (j + (j >= me).astype(jnp.int32), grp)
        remote(stats.at[me], stats.at[me], stat_send, stat_recv, device).start()

    each(n_dp - 1, send_stats)

    def tell_plane(k):
        pl.semaphore_signal(plane_sem, inc=1, device_id=group_member(k), device_id_type=MESH)

    each(n_grp - 1, tell_plane)

    raw = project(2 * CHUNKS, qx, qw, [()] * CHUNKS)
    queries = (raw * lax.rsqrt(jnp.sum(raw * raw, axis=1, keepdims=True) + 1e-06)).astype(
        jnp.bfloat16
    )
    group_queries[grp] = queries

    def query_copy(k):
        return remote(
            group_queries.at[grp],
            group_queries.at[grp],
            query_send,
            query_recv.at[k],
            group_member(k),
        )

    each(n_grp - 1, lambda k: query_copy(k).start())

    positives_load.wait()
    each(
        n_grp - 1,
        lambda k: remote(
            group_positives.at[grp], group_positives.at[grp], pos_send, pos_recv, group_member(k)
        ).start(),
    )

    queue_load.wait()
    pointer_load.wait()
    masks_load.wait()
    pointer = pointer_here[0]
    queue_slots = queue_rows * n_grp
    tile = min(256, queue_rows)

    def queue_sum(batch):
        def step(index, carry):
            start = pl.multiple_of(index * tile, tile)
            scores = temper * times_transposed(slots[pl.ds(start, tile), :], batch)
            slot = lax.broadcasted_iota(jnp.int32, (tile, 1), 0) + (
                grp * queue_rows + start - pointer
            )
            slot = jnp.where(slot < 0, slot + queue_slots, slot)
            kept = jnp.where(slot < columns, 0.0, jnp.exp(scores))
            return carry + jnp.sum(kept.reshape(tile // 8, 8, rows), axis=0)

        count = queue_rows // tile
        total = lax.fori_loop(
            0,
            count,
            step,
            jnp.zeros((8, rows), jnp.float32),
            unroll=count if count <= 8 else 1,
        )
        return jnp.sum(total, axis=0, keepdims=True)

    queue_sums[grp] = queue_sum(queries)

    def whole(send, recv, ref, count):
        span = ref.at[pl.ds(0, count)]
        return remote(span, span, send, recv, neighbour)

    whole(stat_send, stat_recv, stats, n_dp - 1).wait_recv()

    def unpack(i):
        row = stats[i].astype(jnp.float32)
        means[i] = row[:subs] + jnp.where(first_row, 0.0, row[:1])
        scatters[i] = row[subs:]

    each(n_dp, unpack)

    masks = [masks_here[s] for s in range(subs)]
    sublane = lax.broadcasted_iota(jnp.int32, (subs, width), 0)
    keys = []
    for s in range(subs):
        group = me ^ masks[s]
        middle = means[group ^ masks[0]]
        scatter = scatters[group ^ masks[0]]
        for t in range(1, subs):
            here = sublane == t
            middle = jnp.where(here, means[group ^ masks[t]], middle)
            scatter = jnp.where(here, scatters[group ^ masks[t]], scatter)
        centre = jnp.sum(middle, axis=0, keepdims=True) / subs
        middle = middle - centre
        spread = jnp.sum(scatter + middle * middle, axis=0, keepdims=True) / subs
        normed = (projected[pl.ds(s * sub, sub), :] - centre) * lax.rsqrt(spread + epsilon)
        length = jnp.sum(normed * normed, axis=1, keepdims=True)
        keys.append((normed * lax.rsqrt(length + 1e-06)).astype(jnp.bfloat16))
    keys = jnp.concatenate(keys, axis=0)

    def partner_sum(k):
        query_copy(k).wait_recv()
        source = lax.rem(grp + n_grp - (k + 1), n_grp)
        queue_sums[source] = queue_sum(group_queries[source])

    for k in range(n_grp - 1):
        partner_sum(k)
    if n_grp > 1:
        others = group_positives.at[pl.ds(0, n_grp - 1)]
        remote(others, others, pos_send, pos_recv, neighbour).wait_recv()

    inner = temper * times_transposed(keys, group_queries[...].reshape(columns, width))
    wanted = jnp.concatenate([group_positives[g] for g in range(n_grp)], axis=1)
    position = lax.broadcasted_iota(jnp.int32, (rows, 1), 0) + grp * rows
    match = jnp.sum(jnp.where(position == wanted, inner, 0.0), axis=0, keepdims=True)
    total = jnp.sum(jnp.exp(inner), axis=0, keepdims=True) + jnp.concatenate(
        [queue_sums[g] for g in range(n_grp)], axis=1
    )
    match_sum = match[:, :rows]
    for g in range(1, n_grp):
        match_sum = match_sum + match[:, g * rows : (g + 1) * rows]
    own = grp * n_dp + me
    totals[own] = jnp.concatenate([total, match_sum], axis=1)
    matches[grp] = match

    if n_grp > 1:
        pl.semaphore_wait(plane_sem, n_grp - 1)

    def total_copy(device):
        remote(totals.at[own], totals.at[own], total_send, total_recv, device).start()

    def to_row(i):
        row = i + (i >= me).astype(jnp.int32)
        each(n_grp, lambda g: total_copy((row, lax.rem(grp + g, n_grp))))

    each(n_dp - 1, to_row)
    each(n_grp - 1, lambda k: total_copy(group_member(k)))
    each(
        n_grp - 1,
        lambda k: remote(
            matches.at[grp], matches.at[grp], match_send, match_recv, group_member(k)
        ).start(),
    )

    whole(stat_send, stat_recv, stats, n_dp - 1).wait_send()
    if n_grp > 1:
        remote(others, others, pos_send, pos_recv, neighbour).wait_send()
        whole(query_send, query_recv.at[0], group_queries, n_grp - 1).wait_send()
        whole(match_send, match_recv, matches, n_grp - 1).wait_recv()
        whole(match_send, match_recv, matches, n_grp - 1).wait_send()
    whole(total_send, total_recv, totals, n_all - 1).wait_send()
    whole(total_send, total_recv, totals, n_all - 1).wait_recv()

    span = pl.ds(pl.multiple_of(grp * rows, rows), rows)
    own_total = totals[me, :, span]
    own_match = matches[0, :, span]
    gathered = totals[pl.ds(0, n_dp)]
    for g in range(1, n_grp):
        own_total = own_total + totals[g * n_dp + me, :, span]
        own_match = own_match + matches[g, :, span]
        gathered = gathered + totals[pl.ds(g * n_dp, n_dp)]
    result[pl.ds(0, 1), :] = jnp.log(own_total) - own_match
    gathered = gathered.reshape(n_dp, columns + rows)
    logs = jnp.sum(jnp.log(gathered[:, :columns]), axis=0, keepdims=True)
    found = jnp.sum(gathered[:, columns:], axis=0, keepdims=True)
    mean = (jnp.sum(logs, axis=1, keepdims=True) - jnp.sum(found, axis=1, keepdims=True)) / (
        rows * n_all
    )
    result[pl.ds(1, 1), :] = jnp.broadcast_to(mean, (1, rows))


def finish(result, losses, mean_loss):
    losses[...] = result[pl.ds(0, 1), :]
    mean_loss[...] = result[pl.ds(1, 1), pl.ds(0, 1)]


def body(
    n_dp,
    n_grp,
    key_inputs,
    query_inputs,
    key_weight,
    query_weight,
    queue,
    shuffle_masks,
    write_pointer,
    positives,
):
    rows, d_in = key_inputs.shape
    width = key_weight.shape[1]
    subs = shuffle_masks.shape[0]
    columns = rows * n_grp
    dma = pltpu.SemaphoreType.DMA
    vector = pl.BlockSpec(memory_space=pltpu.VMEM)
    result = pl.pallas_call(
        functools.partial(kernel, n_dp, n_grp),
        out_shape=pltpu.VMEM((2, rows), jnp.float32),
        in_specs=[pl.BlockSpec(memory_space=pltpu.HBM)] * 8,
        out_specs=vector,
        scratch_shapes=[
            pltpu.VMEM((rows, d_in), jnp.bfloat16),
            pltpu.VMEM((d_in, width), jnp.bfloat16),
            pltpu.VMEM((rows, d_in), jnp.bfloat16),
            pltpu.VMEM((d_in, width), jnp.bfloat16),
            pltpu.VMEM(queue.shape, jnp.bfloat16),
            pltpu.VMEM((rows, width), jnp.float32),
            pltpu.VMEM((n_dp, 2 * subs, width), jnp.bfloat16),
            pltpu.VMEM((n_dp, subs, width), jnp.float32),
            pltpu.VMEM((n_dp, subs, width), jnp.float32),
            pltpu.VMEM((n_grp, rows, width), jnp.bfloat16),
            pltpu.VMEM((n_grp, 1, rows), jnp.int32),
            pltpu.VMEM((n_grp, 1, rows), jnp.float32),
            pltpu.VMEM((n_grp * n_dp, 1, columns + rows), jnp.float32),
            pltpu.VMEM((n_grp, 1, columns), jnp.float32),
            pltpu.SMEM((subs,), jnp.int32),
            pltpu.SMEM((1,), jnp.int32),
            dma((4 * CHUNKS + 4,)),
            dma,
            dma,
            dma,
            dma((n_grp,)),
            dma,
            dma,
            dma,
            dma,
            dma,
            dma,
            pltpu.SemaphoreType.REGULAR,
        ],
        compiler_params=pltpu.CompilerParams(
            collective_id=0, has_side_effects=True, vmem_limit_bytes=56 * 2**20
        ),
        name="contrast",
    )(
        key_inputs,
        query_inputs,
        key_weight,
        query_weight,
        queue,
        shuffle_masks,
        write_pointer,
        positives.reshape(1, rows),
    )
    losses, mean_loss = pl.pallas_call(
        finish,
        out_shape=(
            jax.ShapeDtypeStruct((1, rows), jnp.float32),
            jax.ShapeDtypeStruct((1, 1), jnp.float32),
        ),
        in_specs=[vector],
        out_specs=(vector, vector),
        compiler_params=pltpu.CompilerParams(vmem_limit_bytes=2**20),
        name="finish",
    )(result)
    return losses.reshape(rows), mean_loss.reshape(1)


def solution(mesh):
    placed = (
        P(("dp", "grp"), None),
        P(("dp", "grp"), None),
        P(),
        P(),
        P("grp", None),
        P(),
        P(),
        P(("dp", "grp")),
    )
    return jax.shard_map(
        functools.partial(body, mesh.shape["dp"], mesh.shape["grp"]),
        mesh=mesh,
        in_specs=placed,
        out_specs=(P(("dp", "grp")), P()),
        check_vma=False,
    )
```

```python
import functools

import jax
import jax.numpy as jnp
from jax import lax
from jax.experimental import pallas as pl
from jax.experimental.pallas import tpu as pltpu
from jax.sharding import PartitionSpec as P

epsilon = 1e-05
temper = 5.0
MESH = pl.DeviceIdType.MESH
CHUNKS = 4
FIRST = 2
DIRECT = 1


def each(count, body):
    def step(index, carry):
        body(index)
        return carry

    if count > 0:
        lax.fori_loop(0, count, step, 0, unroll=count if count <= 32 else 1)


def times_transposed(left, right):
    return lax.dot_general(
        left, right, (((1,), (1,)), ((), ())), preferred_element_type=jnp.float32
    )


def kernel(
    n_dp,
    n_grp,
    key_inputs,
    query_inputs,
    key_weight,
    query_weight,
    queue,
    shuffle_masks,
    write_pointer,
    positives,
    result,
    kx,
    kw,
    qx,
    qw,
    slots,
    projected,
    stats,
    means,
    scatters,
    group_queries,
    group_positives,
    queue_sums,
    totals,
    matches,
    masks_here,
    pointer_here,
    local_sem,
    stat_send,
    stat_recv,
    relay_send,
    relay_recv,
    query_send,
    query_recv,
    pos_send,
    pos_recv,
    total_send,
    total_recv,
    match_send,
    match_recv,
    plane_sem,
    core_sem,
):
    d_in, width = kw.shape
    rows = kx.shape[0]
    subs = means.shape[1]
    sub = rows // subs
    part = d_in // CHUNKS
    queue_rows = slots.shape[0]
    columns = n_grp * rows
    n_chips = n_dp // 2
    n_all = n_dp * n_grp
    me = lax.axis_index("dp")
    grp = lax.axis_index("grp")
    core = lax.rem(me, 2)
    chip = lax.div(me, 2)
    direct = min(DIRECT, n_chips)
    last = chip >= n_chips - direct
    neighbour = (me ^ 1, grp)

    barrier = pltpu.get_barrier_semaphore()

    def greet(device):
        pl.semaphore_signal(barrier, inc=1, device_id=device, device_id_type=MESH)

    def group_member(k):
        return (me, lax.rem(grp + 1 + k, n_grp))

    loads = []
    for x_hbm, x, w_hbm, w in (
        (key_inputs, kx, key_weight, kw),
        (query_inputs, qx, query_weight, qw),
    ):
        for c in range(CHUNKS):
            span = pl.ds(c * part, part)
            loads.append((x_hbm.at[:, span], x.at[:, span]))
            loads.append((w_hbm.at[span, :], w.at[span, :]))
    loads.append((queue, slots))
    loads.append((positives, group_positives.at[grp]))
    loads.append((shuffle_masks, masks_here))
    loads.append((write_pointer, pointer_here))
    loads = [
        pltpu.make_async_copy(source, target, local_sem.at[index])
        for index, (source, target) in enumerate(loads)
    ]
    for load in loads[:FIRST]:
        load.start()
    queue_load, positives_load, masks_load, pointer_load = loads[-4:]
    def other_chip(i):
        return i + (i >= chip).astype(jnp.int32)

    def greet_chip(i):
        target = other_chip(i)
        greet((target * 2 + core, grp))

        @pl.when(last)
        def _():
            greet((target * 2 + 1 - core, grp))

    each(n_chips - 1, greet_chip)
    each(n_grp - 1, lambda k: greet(group_member(k)))
    greet(neighbour)
    for load in loads[FIRST:]:
        load.start()

    def project(first, x, w, later):
        total = None
        for c in range(CHUNKS):
            loads[first + 2 * c].wait()
            loads[first + 2 * c + 1].wait()
            for load in later[c]:
                load.start()
            span = pl.ds(c * part, part)
            term = jnp.dot(x[:, span], w[span, :], preferred_element_type=jnp.float32)
            total = term if total is None else total + term
        return total

    keys_raw = project(0, kx, kw, [()] * CHUNKS)
    projected[...] = keys_raw
    blocks = keys_raw.reshape(subs, sub, width)
    centres = jnp.sum(blocks, axis=1) / sub
    apart = blocks - centres[:, None, :]
    base = centres[:1].astype(jnp.bfloat16)
    first_row = lax.broadcasted_iota(jnp.int32, (subs, width), 0) == 0
    coded = jnp.where(first_row, centres, centres - base.astype(jnp.float32))
    stats[me] = jnp.concatenate(
        [coded, jnp.sum(apart * apart, axis=1) / sub], axis=0
    ).astype(jnp.bfloat16)

    pl.semaphore_wait(barrier, n_chips + n_grp - 1 + direct - last.astype(jnp.int32))

    def remote(source, target, send, recv, device):
        return pltpu.make_async_remote_copy(
            src_ref=source,
            dst_ref=target,
            send_sem=send,
            recv_sem=recv,
            device_id=device,
            device_id_type=MESH,
        )

    def relay_copy(slot, device):
        return remote(stats.at[slot], stats.at[slot], relay_send, relay_recv, device)

    def stat_copy(target):
        device = (target * 2 + core, grp)
        return remote(stats.at[me], stats.at[me], stat_send, stat_recv.at[target ^ chip], device)

    def send_stats(i):
        target = other_chip(n_chips - 2 - i)
        stat_copy(target).start()

        @pl.when(target >= n_chips - direct)
        def _():
            relay_copy(me, (target * 2 + 1 - core, grp)).start()

    each(n_chips - 1, send_stats)
    relay_copy(me, neighbour).start()

    def tell_plane(k):
        pl.semaphore_signal(plane_sem, inc=1, device_id=group_member(k), device_id_type=MESH)

    each(n_grp - 1, tell_plane)

    raw = project(2 * CHUNKS, qx, qw, [()] * CHUNKS)
    queries = (raw * lax.rsqrt(jnp.sum(raw * raw, axis=1, keepdims=True) + 1e-06)).astype(
        jnp.bfloat16
    )
    group_queries[grp] = queries

    def query_copy(k):
        return remote(
            group_queries.at[grp],
            group_queries.at[grp],
            query_send,
            query_recv.at[k],
            group_member(k),
        )

    each(n_grp - 1, lambda k: query_copy(k).start())

    positives_load.wait()
    each(
        n_grp - 1,
        lambda k: remote(
            group_positives.at[grp], group_positives.at[grp], pos_send, pos_recv, group_member(k)
        ).start(),
    )

    if n_grp > 1:
        pl.semaphore_wait(plane_sem, n_grp - 1)
    pl.semaphore_signal(core_sem, inc=1, device_id=neighbour, device_id_type=MESH)

    queue_load.wait()
    pointer_load.wait()
    masks_load.wait()
    pointer = pointer_here[0]
    queue_slots = queue_rows * n_grp
    tile = min(256, queue_rows)

    def queue_sum(batch):
        def step(index, carry):
            start = pl.multiple_of(index * tile, tile)
            scores = temper * times_transposed(slots[pl.ds(start, tile), :], batch)
            slot = lax.broadcasted_iota(jnp.int32, (tile, 1), 0) + (
                grp * queue_rows + start - pointer
            )
            slot = jnp.where(slot < 0, slot + queue_slots, slot)
            kept = jnp.where(slot < columns, 0.0, jnp.exp(scores))
            return carry + jnp.sum(kept.reshape(tile // 8, 8, rows), axis=0)

        count = queue_rows // tile
        total = lax.fori_loop(
            0,
            count,
            step,
            jnp.zeros((8, rows), jnp.float32),
            unroll=count if count <= 8 else 1,
        )
        return jnp.sum(total, axis=0, keepdims=True)

    queue_sums[grp] = queue_sum(queries)

    def pass_on(i):
        source = other_chip(i)
        stat_copy(source).wait_recv()

        @pl.when(jnp.logical_not(last))
        def _():
            relay_copy(source * 2 + core, neighbour).start()

    def partner_sum(k):
        query_copy(k).wait_recv()
        source = lax.rem(grp + n_grp - (k + 1), n_grp)
        queue_sums[source] = queue_sum(group_queries[source])

    def partner_sums():
        for k in range(n_grp - 1):
            partner_sum(k)

    pl.when(grp > 0)(partner_sums)
    each(n_chips - 1, pass_on)

    def whole(send, recv, ref, count):
        span = ref.at[pl.ds(0, count)]
        return remote(span, span, send, recv, neighbour)


    whole(relay_send, relay_recv, stats, n_chips).wait_recv()

    def unpack(i):
        row = stats[i].astype(jnp.float32)
        means[i] = row[:subs] + jnp.where(first_row, 0.0, row[:1])
        scatters[i] = row[subs:]

    each(n_dp, unpack)

    masks = [masks_here[s] for s in range(subs)]
    sublane = lax.broadcasted_iota(jnp.int32, (subs, width), 0)
    keys = []
    for s in range(subs):
        group = me ^ masks[s]
        middle = means[group ^ masks[0]]
        scatter = scatters[group ^ masks[0]]
        for t in range(1, subs):
            here = sublane == t
            middle = jnp.where(here, means[group ^ masks[t]], middle)
            scatter = jnp.where(here, scatters[group ^ masks[t]], scatter)
        centre = jnp.sum(middle, axis=0, keepdims=True) / subs
        middle = middle - centre
        spread = jnp.sum(scatter + middle * middle, axis=0, keepdims=True) / subs
        normed = (projected[pl.ds(s * sub, sub), :] - centre) * lax.rsqrt(spread + epsilon)
        length = jnp.sum(normed * normed, axis=1, keepdims=True)
        keys.append((normed * lax.rsqrt(length + 1e-06)).astype(jnp.bfloat16))
    keys = jnp.concatenate(keys, axis=0)

    pl.when(grp == 0)(partner_sums)
    if n_grp > 1:
        others = group_positives.at[pl.ds(0, n_grp - 1)]
        remote(others, others, pos_send, pos_recv, neighbour).wait_recv()

    inner = temper * times_transposed(keys, group_queries[...].reshape(columns, width))
    wanted = jnp.concatenate([group_positives[g] for g in range(n_grp)], axis=1)
    position = lax.broadcasted_iota(jnp.int32, (rows, 1), 0) + grp * rows
    match = jnp.sum(jnp.where(position == wanted, inner, 0.0), axis=0, keepdims=True)
    total = jnp.sum(jnp.exp(inner), axis=0, keepdims=True) + jnp.concatenate(
        [queue_sums[g] for g in range(n_grp)], axis=1
    )
    match_sum = match[:, :rows]
    for g in range(1, n_grp):
        match_sum = match_sum + match[:, g * rows : (g + 1) * rows]
    own = grp * n_dp + me
    totals[own] = jnp.concatenate([total, match_sum], axis=1)
    matches[grp] = match

    pl.semaphore_wait(core_sem, 1)

    def total_copy(device):
        remote(totals.at[own], totals.at[own], total_send, total_recv, device).start()

    def to_row(i):
        row = i + (i >= me).astype(jnp.int32)
        each(n_grp, lambda g: total_copy((row, lax.rem(grp + g, n_grp))))

    each(n_dp - 1, to_row)
    each(n_grp - 1, lambda k: total_copy(group_member(k)))
    each(
        n_grp - 1,
        lambda k: remote(
            matches.at[grp], matches.at[grp], match_send, match_recv, group_member(k)
        ).start(),
    )

    if n_chips > 1:
        whole(stat_send, relay_recv, stats, n_chips - 1).wait_send()
    @pl.when(last)
    def _():
        whole(relay_send, relay_recv, stats, direct).wait_send()

    @pl.when(jnp.logical_not(last))
    def _():
        whole(relay_send, relay_recv, stats, n_chips).wait_send()
        whole(relay_send, relay_recv, stats, direct).wait_send()

    if n_grp > 1:
        remote(others, others, pos_send, pos_recv, neighbour).wait_send()
        whole(query_send, query_recv.at[0], group_queries, n_grp - 1).wait_send()
        whole(match_send, match_recv, matches, n_grp - 1).wait_recv()
        whole(match_send, match_recv, matches, n_grp - 1).wait_send()
    whole(total_send, total_recv, totals, n_all - 1).wait_send()
    whole(total_send, total_recv, totals, n_all - 1).wait_recv()

    span = pl.ds(pl.multiple_of(grp * rows, rows), rows)
    own_total = totals[me, :, span]
    own_match = matches[0, :, span]
    gathered = totals[pl.ds(0, n_dp)]
    for g in range(1, n_grp):
        own_total = own_total + totals[g * n_dp + me, :, span]
        own_match = own_match + matches[g, :, span]
        gathered = gathered + totals[pl.ds(g * n_dp, n_dp)]
    result[pl.ds(0, 1), :] = jnp.log(own_total) - own_match
    gathered = gathered.reshape(n_dp, columns + rows)
    logs = jnp.sum(jnp.log(gathered[:, :columns]), axis=0, keepdims=True)
    found = jnp.sum(gathered[:, columns:], axis=0, keepdims=True)
    mean = (jnp.sum(logs, axis=1, keepdims=True) - jnp.sum(found, axis=1, keepdims=True)) / (
        rows * n_all
    )
    result[pl.ds(1, 1), :] = jnp.broadcast_to(mean, (1, rows))


def finish(result, losses, mean_loss):
    losses[...] = result[pl.ds(0, 1), :]
    mean_loss[...] = result[pl.ds(1, 1), pl.ds(0, 1)]


def body(
    n_dp,
    n_grp,
    key_inputs,
    query_inputs,
    key_weight,
    query_weight,
    queue,
    shuffle_masks,
    write_pointer,
    positives,
):
    rows, d_in = key_inputs.shape
    width = key_weight.shape[1]
    subs = shuffle_masks.shape[0]
    columns = rows * n_grp
    dma = pltpu.SemaphoreType.DMA
    vector = pl.BlockSpec(memory_space=pltpu.VMEM)
    result = pl.pallas_call(
        functools.partial(kernel, n_dp, n_grp),
        out_shape=pltpu.VMEM((2, rows), jnp.float32),
        in_specs=[pl.BlockSpec(memory_space=pltpu.HBM)] * 8,
        out_specs=vector,
        scratch_shapes=[
            pltpu.VMEM((rows, d_in), jnp.bfloat16),
            pltpu.VMEM((d_in, width), jnp.bfloat16),
            pltpu.VMEM((rows, d_in), jnp.bfloat16),
            pltpu.VMEM((d_in, width), jnp.bfloat16),
            pltpu.VMEM(queue.shape, jnp.bfloat16),
            pltpu.VMEM((rows, width), jnp.float32),
            pltpu.VMEM((n_dp, 2 * subs, width), jnp.bfloat16),
            pltpu.VMEM((n_dp, subs, width), jnp.float32),
            pltpu.VMEM((n_dp, subs, width), jnp.float32),
            pltpu.VMEM((n_grp, rows, width), jnp.bfloat16),
            pltpu.VMEM((n_grp, 1, rows), jnp.int32),
            pltpu.VMEM((n_grp, 1, rows), jnp.float32),
            pltpu.VMEM((n_grp * n_dp, 1, columns + rows), jnp.float32),
            pltpu.VMEM((n_grp, 1, columns), jnp.float32),
            pltpu.SMEM((subs,), jnp.int32),
            pltpu.SMEM((1,), jnp.int32),
            dma((4 * CHUNKS + 4,)),
            dma,
            dma((n_dp // 2,)),
            dma,
            dma,
            dma,
            dma((n_grp,)),
            dma,
            dma,
            dma,
            dma,
            dma,
            dma,
            pltpu.SemaphoreType.REGULAR,
            pltpu.SemaphoreType.REGULAR,
        ],
        compiler_params=pltpu.CompilerParams(
            collective_id=0, has_side_effects=True, vmem_limit_bytes=56 * 2**20
        ),
        name="contrast",
    )(
        key_inputs,
        query_inputs,
        key_weight,
        query_weight,
        queue,
        shuffle_masks,
        write_pointer,
        positives.reshape(1, rows),
    )
    losses, mean_loss = pl.pallas_call(
        finish,
        out_shape=(
            jax.ShapeDtypeStruct((1, rows), jnp.float32),
            jax.ShapeDtypeStruct((1, 1), jnp.float32),
        ),
        in_specs=[vector],
        out_specs=(vector, vector),
        compiler_params=pltpu.CompilerParams(vmem_limit_bytes=2**20),
        name="finish",
    )(result)
    return losses.reshape(rows), mean_loss.reshape(1)


def solution(mesh):
    placed = (
        P(("dp", "grp"), None),
        P(("dp", "grp"), None),
        P(),
        P(),
        P("grp", None),
        P(),
        P(),
        P(("dp", "grp")),
    )
    return jax.shard_map(
        functools.partial(body, mesh.shape["dp"], mesh.shape["grp"]),
        mesh=mesh,
        in_specs=placed,
        out_specs=(P(("dp", "grp")), P()),
        check_vma=False,
    )
```

```python
import functools

import jax
import jax.numpy as jnp
from jax import lax
from jax.experimental import pallas as pl
from jax.experimental.pallas import tpu as pltpu
from jax.sharding import PartitionSpec as P

epsilon = 1e-05
temper = 5.0
MESH = pl.DeviceIdType.MESH
CHUNKS = 4
FIRST = 2
DIRECT = 1


def each(count, body):
    def step(index, carry):
        body(index)
        return carry

    if count > 0:
        lax.fori_loop(0, count, step, 0, unroll=count if count <= 32 else 1)


def times_transposed(left, right):
    return lax.dot_general(
        left, right, (((1,), (1,)), ((), ())), preferred_element_type=jnp.float32
    )


def kernel(
    n_dp,
    n_grp,
    key_inputs,
    query_inputs,
    key_weight,
    query_weight,
    queue,
    shuffle_masks,
    write_pointer,
    positives,
    result,
    kx,
    kw,
    qx,
    qw,
    slots,
    projected,
    stats,
    means,
    scatters,
    group_queries,
    group_positives,
    queue_sums,
    totals,
    matches,
    masks_here,
    pointer_here,
    local_sem,
    stat_send,
    stat_recv,
    relay_send,
    relay_recv,
    query_send,
    query_recv,
    pos_send,
    pos_recv,
    total_send,
    total_recv,
    match_send,
    match_recv,
    plane_sem,
    core_sem,
):
    d_in, width = kw.shape
    rows = kx.shape[0]
    subs = means.shape[1]
    sub = rows // subs
    part = d_in // CHUNKS
    queue_rows = slots.shape[0]
    columns = n_grp * rows
    n_chips = n_dp // 2
    n_all = n_dp * n_grp
    me = lax.axis_index("dp")
    grp = lax.axis_index("grp")
    core = lax.rem(me, 2)
    chip = lax.div(me, 2)
    direct = min(DIRECT, n_chips)
    last = chip >= n_chips - direct
    neighbour = (me ^ 1, grp)

    barrier = pltpu.get_barrier_semaphore()

    def greet(device):
        pl.semaphore_signal(barrier, inc=1, device_id=device, device_id_type=MESH)

    def group_member(k):
        return (me, lax.rem(grp + 1 + k, n_grp))

    loads = []
    for x_hbm, x, w_hbm, w in (
        (key_inputs, kx, key_weight, kw),
        (query_inputs, qx, query_weight, qw),
    ):
        for c in range(CHUNKS):
            span = pl.ds(c * part, part)
            loads.append((x_hbm.at[:, span], x.at[:, span]))
            loads.append((w_hbm.at[span, :], w.at[span, :]))
    loads.append((queue, slots))
    loads.append((positives, group_positives.at[grp]))
    loads.append((shuffle_masks, masks_here))
    loads.append((write_pointer, pointer_here))
    loads = [
        pltpu.make_async_copy(source, target, local_sem.at[index])
        for index, (source, target) in enumerate(loads)
    ]
    for load in loads[:FIRST]:
        load.start()
    queue_load, positives_load, masks_load, pointer_load = loads[-4:]
    def other_chip(i):
        return i + (i >= chip).astype(jnp.int32)

    def greet_chip(i):
        target = other_chip(i)
        greet((target * 2 + core, grp))

        @pl.when(last)
        def _():
            greet((target * 2 + 1 - core, grp))

    each(n_chips - 1, greet_chip)
    each(n_grp - 1, lambda k: greet(group_member(k)))
    greet(neighbour)
    for load in loads[FIRST:]:
        load.start()

    def project(first, x, w, later):
        total = None
        for c in range(CHUNKS):
            loads[first + 2 * c].wait()
            loads[first + 2 * c + 1].wait()
            for load in later[c]:
                load.start()
            span = pl.ds(c * part, part)
            term = jnp.dot(x[:, span], w[span, :], preferred_element_type=jnp.float32)
            total = term if total is None else total + term
        return total

    keys_raw = project(0, kx, kw, [()] * CHUNKS)
    projected[...] = keys_raw
    blocks = keys_raw.reshape(subs, sub, width)
    centres = jnp.sum(blocks, axis=1) / sub
    apart = blocks - centres[:, None, :]
    base = centres[:1].astype(jnp.bfloat16)
    first_row = lax.broadcasted_iota(jnp.int32, (subs, width), 0) == 0
    coded = jnp.where(first_row, centres, centres - base.astype(jnp.float32))
    stats[core, chip] = jnp.concatenate(
        [coded, jnp.sum(apart * apart, axis=1) / sub], axis=0
    ).astype(jnp.bfloat16)

    pl.semaphore_wait(barrier, n_chips + n_grp - 1 + direct - last.astype(jnp.int32))

    def remote(source, target, send, recv, device):
        return pltpu.make_async_remote_copy(
            src_ref=source,
            dst_ref=target,
            send_sem=send,
            recv_sem=recv,
            device_id=device,
            device_id_type=MESH,
        )

    def whole(send, recv, ref, count):
        span = ref.at[pl.ds(0, count)]
        return remote(span, span, send, recv, neighbour)


    own_stats = stats.at[core, chip]

    def send_stats(i):
        target = other_chip(n_chips - 2 - i)
        remote(own_stats, own_stats, stat_send, stat_recv, (target * 2 + core, grp)).start()

        @pl.when(target >= n_chips - direct)
        def _():
            device = (target * 2 + 1 - core, grp)
            remote(own_stats, own_stats, stat_send, relay_recv, device).start()

    each(n_chips - 1, send_stats)

    @pl.when(last)
    def _():
        remote(own_stats, own_stats, relay_send, relay_recv, neighbour).start()

    def tell_plane(k):
        pl.semaphore_signal(plane_sem, inc=1, device_id=group_member(k), device_id_type=MESH)

    each(n_grp - 1, tell_plane)

    raw = project(2 * CHUNKS, qx, qw, [()] * CHUNKS)
    queries = (raw * lax.rsqrt(jnp.sum(raw * raw, axis=1, keepdims=True) + 1e-06)).astype(
        jnp.bfloat16
    )
    group_queries[grp] = queries

    def query_copy(k):
        return remote(
            group_queries.at[grp],
            group_queries.at[grp],
            query_send,
            query_recv.at[k],
            group_member(k),
        )

    each(n_grp - 1, lambda k: query_copy(k).start())

    positives_load.wait()
    each(
        n_grp - 1,
        lambda k: remote(
            group_positives.at[grp], group_positives.at[grp], pos_send, pos_recv, group_member(k)
        ).start(),
    )

    if n_grp > 1:
        pl.semaphore_wait(plane_sem, n_grp - 1)
    pl.semaphore_signal(core_sem, inc=1, device_id=neighbour, device_id_type=MESH)

    queue_load.wait()
    pointer_load.wait()
    masks_load.wait()
    pointer = pointer_here[0]
    queue_slots = queue_rows * n_grp
    tile = min(256, queue_rows)

    def queue_sum(batch):
        def step(index, carry):
            start = pl.multiple_of(index * tile, tile)
            scores = temper * times_transposed(slots[pl.ds(start, tile), :], batch)
            slot = lax.broadcasted_iota(jnp.int32, (tile, 1), 0) + (
                grp * queue_rows + start - pointer
            )
            slot = jnp.where(slot < 0, slot + queue_slots, slot)
            kept = jnp.where(slot < columns, 0.0, jnp.exp(scores))
            return carry + jnp.sum(kept.reshape(tile // 8, 8, rows), axis=0)

        count = queue_rows // tile
        total = lax.fori_loop(
            0,
            count,
            step,
            jnp.zeros((8, rows), jnp.float32),
            unroll=count if count <= 8 else 1,
        )
        return jnp.sum(total, axis=0, keepdims=True)

    queue_sums[grp] = queue_sum(queries)

    def pass_on():
        if n_chips > 1:
            whole(stat_send, stat_recv, stats.at[0], n_chips - 1).wait_recv()

        @pl.when(jnp.logical_not(last))
        def _():
            remote(stats.at[core], stats.at[core], relay_send, relay_recv, neighbour).start()

    def partner_sum(k):
        query_copy(k).wait_recv()
        source = lax.rem(grp + n_grp - (k + 1), n_grp)
        queue_sums[source] = queue_sum(group_queries[source])

    def partner_sums():
        for k in range(n_grp - 1):
            partner_sum(k)

    pl.when(grp > 0)(partner_sums)
    pass_on()

    whole(relay_send, relay_recv, stats.at[0], n_chips).wait_recv()

    def unpack(i):
        row = stats[lax.rem(i, 2), lax.div(i, 2)].astype(jnp.float32)
        means[i] = row[:subs] + jnp.where(first_row, 0.0, row[:1])
        scatters[i] = row[subs:]

    each(n_dp, unpack)

    masks = [masks_here[s] for s in range(subs)]
    sublane = lax.broadcasted_iota(jnp.int32, (subs, width), 0)
    keys = []
    for s in range(subs):
        group = me ^ masks[s]
        middle = means[group ^ masks[0]]
        scatter = scatters[group ^ masks[0]]
        for t in range(1, subs):
            here = sublane == t
            middle = jnp.where(here, means[group ^ masks[t]], middle)
            scatter = jnp.where(here, scatters[group ^ masks[t]], scatter)
        centre = jnp.sum(middle, axis=0, keepdims=True) / subs
        middle = middle - centre
        spread = jnp.sum(scatter + middle * middle, axis=0, keepdims=True) / subs
        normed = (projected[pl.ds(s * sub, sub), :] - centre) * lax.rsqrt(spread + epsilon)
        length = jnp.sum(normed * normed, axis=1, keepdims=True)
        keys.append((normed * lax.rsqrt(length + 1e-06)).astype(jnp.bfloat16))
    keys = jnp.concatenate(keys, axis=0)

    own = grp * n_dp + me
    if n_grp > 1:
        others = group_positives.at[pl.ds(0, n_grp - 1)]
        remote(others, others, pos_send, pos_recv, neighbour).wait_recv()

    def finish_totals():
        inner = temper * times_transposed(keys, group_queries[...].reshape(columns, width))
        wanted = jnp.concatenate([group_positives[g] for g in range(n_grp)], axis=1)
        position = lax.broadcasted_iota(jnp.int32, (rows, 1), 0) + grp * rows
        match = jnp.sum(jnp.where(position == wanted, inner, 0.0), axis=0, keepdims=True)
        total = jnp.sum(jnp.exp(inner), axis=0, keepdims=True) + jnp.concatenate(
            [queue_sums[g] for g in range(n_grp)], axis=1
        )
        match_sum = match[:, :rows]
        for g in range(1, n_grp):
            match_sum = match_sum + match[:, g * rows : (g + 1) * rows]
        totals[own] = jnp.concatenate([total, match_sum], axis=1)
        matches[grp] = match

    @pl.when(grp == 0)
    def _():
        partner_sums()
        finish_totals()

    pl.when(grp > 0)(finish_totals)

    pl.semaphore_wait(core_sem, 1)

    def total_copy(device):
        remote(totals.at[own], totals.at[own], total_send, total_recv, device).start()

    def to_row(i):
        row = i + (i >= me).astype(jnp.int32)
        each(n_grp, lambda g: total_copy((row, lax.rem(grp + g, n_grp))))

    each(n_dp - 1, to_row)
    each(n_grp - 1, lambda k: total_copy(group_member(k)))
    each(
        n_grp - 1,
        lambda k: remote(
            matches.at[grp], matches.at[grp], match_send, match_recv, group_member(k)
        ).start(),
    )

    if n_chips > 1:
        whole(stat_send, relay_recv, stats.at[0], n_chips - 1).wait_send()

    @pl.when(last)
    def _():
        whole(relay_send, relay_recv, stats.at[0], 1).wait_send()
        if direct > 1:
            whole(stat_send, relay_recv, stats.at[0], direct - 1).wait_send()

    @pl.when(jnp.logical_not(last))
    def _():
        whole(relay_send, relay_recv, stats.at[0], n_chips).wait_send()
        if direct > 0:
            whole(stat_send, relay_recv, stats.at[0], direct).wait_send()

    if n_grp > 1:
        remote(others, others, pos_send, pos_recv, neighbour).wait_send()
        whole(query_send, query_recv.at[0], group_queries, n_grp - 1).wait_send()
        whole(match_send, match_recv, matches, n_grp - 1).wait_recv()
        whole(match_send, match_recv, matches, n_grp - 1).wait_send()
    whole(total_send, total_recv, totals, n_all - 1).wait_send()
    whole(total_send, total_recv, totals, n_all - 1).wait_recv()

    span = pl.ds(pl.multiple_of(grp * rows, rows), rows)
    own_total = totals[me, :, span]
    own_match = matches[0, :, span]
    gathered = totals[pl.ds(0, n_dp)]
    for g in range(1, n_grp):
        own_total = own_total + totals[g * n_dp + me, :, span]
        own_match = own_match + matches[g, :, span]
        gathered = gathered + totals[pl.ds(g * n_dp, n_dp)]
    result[pl.ds(0, 1), :] = jnp.log(own_total) - own_match
    gathered = gathered.reshape(n_dp, columns + rows)
    logs = jnp.sum(jnp.log(gathered[:, :columns]), axis=0, keepdims=True)
    found = jnp.sum(gathered[:, columns:], axis=0, keepdims=True)
    mean = (jnp.sum(logs, axis=1, keepdims=True) - jnp.sum(found, axis=1, keepdims=True)) / (
        rows * n_all
    )
    result[pl.ds(1, 1), :] = jnp.broadcast_to(mean, (1, rows))


def finish(result, losses, mean_loss):
    losses[...] = result[pl.ds(0, 1), :]
    mean_loss[...] = result[pl.ds(1, 1), pl.ds(0, 1)]


def body(
    n_dp,
    n_grp,
    key_inputs,
    query_inputs,
    key_weight,
    query_weight,
    queue,
    shuffle_masks,
    write_pointer,
    positives,
):
    rows, d_in = key_inputs.shape
    width = key_weight.shape[1]
    subs = shuffle_masks.shape[0]
    columns = rows * n_grp
    dma = pltpu.SemaphoreType.DMA
    vector = pl.BlockSpec(memory_space=pltpu.VMEM)
    result = pl.pallas_call(
        functools.partial(kernel, n_dp, n_grp),
        out_shape=pltpu.VMEM((2, rows), jnp.float32),
        in_specs=[pl.BlockSpec(memory_space=pltpu.HBM)] * 8,
        out_specs=vector,
        scratch_shapes=[
            pltpu.VMEM((rows, d_in), jnp.bfloat16),
            pltpu.VMEM((d_in, width), jnp.bfloat16),
            pltpu.VMEM((rows, d_in), jnp.bfloat16),
            pltpu.VMEM((d_in, width), jnp.bfloat16),
            pltpu.VMEM(queue.shape, jnp.bfloat16),
            pltpu.VMEM((rows, width), jnp.float32),
            pltpu.VMEM((2, n_dp // 2, 2 * subs, width), jnp.bfloat16),
            pltpu.VMEM((n_dp, subs, width), jnp.float32),
            pltpu.VMEM((n_dp, subs, width), jnp.float32),
            pltpu.VMEM((n_grp, rows, width), jnp.bfloat16),
            pltpu.VMEM((n_grp, 1, rows), jnp.int32),
            pltpu.VMEM((n_grp, 1, rows), jnp.float32),
            pltpu.VMEM((n_grp * n_dp, 1, columns + rows), jnp.float32),
            pltpu.VMEM((n_grp, 1, columns), jnp.float32),
            pltpu.SMEM((subs,), jnp.int32),
            pltpu.SMEM((1,), jnp.int32),
            dma((4 * CHUNKS + 4,)),
            dma,
            dma,
            dma,
            dma,
            dma,
            dma((n_grp,)),
            dma,
            dma,
            dma,
            dma,
            dma,
            dma,
            pltpu.SemaphoreType.REGULAR,
            pltpu.SemaphoreType.REGULAR,
        ],
        compiler_params=pltpu.CompilerParams(
            collective_id=0, has_side_effects=True, vmem_limit_bytes=56 * 2**20
        ),
        name="contrast",
    )(
        key_inputs,
        query_inputs,
        key_weight,
        query_weight,
        queue,
        shuffle_masks,
        write_pointer,
        positives.reshape(1, rows),
    )
    losses, mean_loss = pl.pallas_call(
        finish,
        out_shape=(
            jax.ShapeDtypeStruct((1, rows), jnp.float32),
            jax.ShapeDtypeStruct((1, 1), jnp.float32),
        ),
        in_specs=[vector],
        out_specs=(vector, vector),
        compiler_params=pltpu.CompilerParams(vmem_limit_bytes=2**20),
        name="finish",
    )(result)
    return losses.reshape(rows), mean_loss.reshape(1)


def solution(mesh):
    placed = (
        P(("dp", "grp"), None),
        P(("dp", "grp"), None),
        P(),
        P(),
        P("grp", None),
        P(),
        P(),
        P(("dp", "grp")),
    )
    return jax.shard_map(
        functools.partial(body, mesh.shape["dp"], mesh.shape["grp"]),
        mesh=mesh,
        in_specs=placed,
        out_specs=(P(("dp", "grp")), P()),
        check_vma=False,
    )
```

```python
import functools
import math

import jax
import jax.numpy as jnp
from jax import lax
from jax.experimental import pallas as pl
from jax.experimental.pallas import tpu as pltpu
from jax.sharding import PartitionSpec as P

epsilon = 1e-05
temper = 5.0
power = temper / math.log(2.0)
MESH = pl.DeviceIdType.MESH
CHUNKS = 4
FIRST = 6
DIRECT = 1


def each(count, body):
    def step(index, carry):
        body(index)
        return carry

    if count > 0:
        lax.fori_loop(0, count, step, 0, unroll=count if count <= 32 else 1)


def times_transposed(left, right):
    return lax.dot_general(
        left, right, (((1,), (1,)), ((), ())), preferred_element_type=jnp.float32
    )


def kernel(
    n_dp,
    n_grp,
    key_inputs,
    query_inputs,
    key_weight,
    query_weight,
    queue,
    shuffle_masks,
    write_pointer,
    positives,
    result,
    kx,
    kw,
    qx,
    qw,
    slots,
    projected,
    stats,
    means,
    scatters,
    group_queries,
    group_positives,
    queue_sums,
    totals,
    matches,
    masks_here,
    pointer_here,
    local_sem,
    stat_send,
    stat_recv,
    relay_send,
    relay_recv,
    query_send,
    query_recv,
    pos_send,
    pos_recv,
    total_send,
    total_recv,
    match_send,
    match_recv,
    plane_sem,
    core_sem,
):
    d_in, width = kw.shape
    rows = kx.shape[0]
    subs = means.shape[1]
    sub = rows // subs
    part = d_in // CHUNKS
    queue_rows = slots.shape[0]
    columns = n_grp * rows
    n_chips = n_dp // 2
    n_all = n_dp * n_grp
    me = lax.axis_index("dp")
    grp = lax.axis_index("grp")
    core = lax.rem(me, 2)
    chip = lax.div(me, 2)
    direct = min(DIRECT, n_chips)
    last = chip >= n_chips - direct
    neighbour = (me ^ 1, grp)

    barrier = pltpu.get_barrier_semaphore()

    def greet(device):
        pl.semaphore_signal(barrier, inc=1, device_id=device, device_id_type=MESH)

    def group_member(k):
        return (me, lax.rem(grp + 1 + k, n_grp))

    loads = []
    for x_hbm, x, w_hbm, w in (
        (key_inputs, kx, key_weight, kw),
        (query_inputs, qx, query_weight, qw),
    ):
        for c in range(CHUNKS):
            span = pl.ds(c * part, part)
            loads.append((x_hbm.at[:, span], x.at[:, span]))
            loads.append((w_hbm.at[span, :], w.at[span, :]))
    loads.append((queue, slots))
    loads.append((positives, group_positives.at[grp]))
    loads.append((shuffle_masks, masks_here))
    loads.append((write_pointer, pointer_here))
    loads = [
        pltpu.make_async_copy(source, target, local_sem.at[index])
        for index, (source, target) in enumerate(loads)
    ]
    for load in loads[:FIRST]:
        load.start()
    queue_load, positives_load, masks_load, pointer_load = loads[-4:]
    def other_chip(i):
        return i + (i >= chip).astype(jnp.int32)

    @pl.when(last)
    def _():
        def greet_both(i):
            greet((other_chip(i) * 2 + core, grp))
            greet((other_chip(i) * 2 + 1 - core, grp))

        each(n_chips - 1, greet_both)

    @pl.when(jnp.logical_not(last))
    def _():
        each(n_chips - 1, lambda i: greet((other_chip(i) * 2 + core, grp)))

    each(n_grp - 1, lambda k: greet(group_member(k)))
    greet(neighbour)
    for load in loads[FIRST:]:
        load.start()

    def project(first, x, w, later):
        total = None
        for c in range(CHUNKS):
            loads[first + 2 * c].wait()
            loads[first + 2 * c + 1].wait()
            for load in later[c]:
                load.start()
            span = pl.ds(c * part, part)
            term = jnp.dot(x[:, span], w[span, :], preferred_element_type=jnp.float32)
            total = term if total is None else total + term
        return total

    keys_raw = project(0, kx, kw, [()] * CHUNKS)
    projected[...] = keys_raw
    blocks = keys_raw.reshape(subs, sub, width)
    centres = jnp.sum(blocks, axis=1) / sub
    apart = blocks - centres[:, None, :]
    base = centres[:1].astype(jnp.bfloat16)
    first_row = lax.broadcasted_iota(jnp.int32, (subs, width), 0) == 0
    coded = jnp.where(first_row, centres, centres - base.astype(jnp.float32))
    stats[core, chip] = jnp.concatenate(
        [coded, jnp.sum(apart * apart, axis=1) / sub], axis=0
    ).astype(jnp.bfloat16)

    pl.semaphore_wait(barrier, n_chips + n_grp - 1 + direct - last.astype(jnp.int32))

    def remote(source, target, send, recv, device):
        return pltpu.make_async_remote_copy(
            src_ref=source,
            dst_ref=target,
            send_sem=send,
            recv_sem=recv,
            device_id=device,
            device_id_type=MESH,
        )

    def whole(send, recv, ref, count):
        span = ref.at[pl.ds(0, count)]
        return remote(span, span, send, recv, neighbour)


    own_stats = stats.at[core, chip]

    def send_direct(i):
        target = n_chips - 1 - i
        for other in range(2):
            device = (target * 2 + (core ^ other), grp)
            arrival = relay_recv if other else stat_recv
            remote(own_stats, own_stats, stat_send, arrival, device).start()

    def send_stats(i):
        target = other_chip(n_chips - 2 - i)
        remote(own_stats, own_stats, stat_send, stat_recv, (target * 2 + core, grp)).start()

    @pl.when(jnp.logical_not(last))
    def _():
        send_direct(0)
        each(n_chips - 2, lambda i: send_stats(i + 1))

    @pl.when(last)
    def _():
        each(n_chips - 1, send_stats)

    @pl.when(last)
    def _():
        remote(own_stats, own_stats, relay_send, relay_recv, neighbour).start()

    def tell_plane(k):
        pl.semaphore_signal(plane_sem, inc=1, device_id=group_member(k), device_id_type=MESH)

    each(n_grp - 1, tell_plane)

    raw = project(2 * CHUNKS, qx, qw, [()] * CHUNKS)
    queries = (raw * lax.rsqrt(jnp.sum(raw * raw, axis=1, keepdims=True) + 1e-06)).astype(
        jnp.bfloat16
    )
    group_queries[grp] = queries

    def query_copy(k):
        return remote(
            group_queries.at[grp],
            group_queries.at[grp],
            query_send,
            query_recv.at[k],
            group_member(k),
        )

    each(n_grp - 1, lambda k: query_copy(k).start())

    positives_load.wait()
    each(
        n_grp - 1,
        lambda k: remote(
            group_positives.at[grp], group_positives.at[grp], pos_send, pos_recv, group_member(k)
        ).start(),
    )

    if n_grp > 1:
        pl.semaphore_wait(plane_sem, n_grp - 1)
    pl.semaphore_signal(core_sem, inc=1, device_id=neighbour, device_id_type=MESH)

    queue_load.wait()
    pointer_load.wait()
    masks_load.wait()
    pointer = pointer_here[0]
    queue_slots = queue_rows * n_grp
    tile = min(256, queue_rows)

    def queue_sum(batch):
        def step(index, carry):
            start = pl.multiple_of(index * tile, tile)
            scores = power * times_transposed(slots[pl.ds(start, tile), :], batch)
            slot = lax.broadcasted_iota(jnp.int32, (tile, 1), 0) + (
                grp * queue_rows + start - pointer
            )
            slot = jnp.where(slot < 0, slot + queue_slots, slot)
            kept = jnp.where(slot < columns, 0.0, jnp.exp2(scores))
            return carry + jnp.sum(kept.reshape(tile // 8, 8, rows), axis=0)

        count = queue_rows // tile
        total = lax.fori_loop(
            0,
            count,
            step,
            jnp.zeros((8, rows), jnp.float32),
            unroll=count if count <= 8 else 1,
        )
        return jnp.sum(total, axis=0, keepdims=True)

    queue_sums[grp] = queue_sum(queries)

    def pass_on():
        if n_chips > 1:
            whole(stat_send, stat_recv, stats.at[0], n_chips - 1).wait_recv()

        @pl.when(jnp.logical_not(last))
        def _():
            remote(stats.at[core], stats.at[core], relay_send, relay_recv, neighbour).start()

    def partner_sum(k):
        query_copy(k).wait_recv()
        source = lax.rem(grp + n_grp - (k + 1), n_grp)
        queue_sums[source] = queue_sum(group_queries[source])

    def partner_sums():
        for k in range(n_grp - 1):
            partner_sum(k)

    pl.when(grp > 0)(partner_sums)
    pass_on()

    whole(relay_send, relay_recv, stats.at[0], n_chips).wait_recv()

    def unpack(i):
        row = stats[lax.rem(i, 2), lax.div(i, 2)].astype(jnp.float32)
        means[i] = row[:subs] + jnp.where(first_row, 0.0, row[:1])
        scatters[i] = row[subs:]

    each(n_dp, unpack)

    masks = [masks_here[s] for s in range(subs)]
    sublane = lax.broadcasted_iota(jnp.int32, (subs, width), 0)
    keys = []
    for s in range(subs):
        group = me ^ masks[s]
        middle = means[group ^ masks[0]]
        scatter = scatters[group ^ masks[0]]
        for t in range(1, subs):
            here = sublane == t
            middle = jnp.where(here, means[group ^ masks[t]], middle)
            scatter = jnp.where(here, scatters[group ^ masks[t]], scatter)
        centre = jnp.sum(middle, axis=0, keepdims=True) / subs
        middle = middle - centre
        spread = jnp.sum(scatter + middle * middle, axis=0, keepdims=True) / subs
        normed = (projected[pl.ds(s * sub, sub), :] - centre) * lax.rsqrt(spread + epsilon)
        length = jnp.sum(normed * normed, axis=1, keepdims=True)
        keys.append((normed * lax.rsqrt(length + 1e-06)).astype(jnp.bfloat16))
    keys = jnp.concatenate(keys, axis=0)

    own = grp * n_dp + me
    if n_grp > 1:
        others = group_positives.at[pl.ds(0, n_grp - 1)]
        remote(others, others, pos_send, pos_recv, neighbour).wait_recv()

    def finish_totals():
        inner = temper * times_transposed(keys, group_queries[...].reshape(columns, width))
        wanted = jnp.concatenate([group_positives[g] for g in range(n_grp)], axis=1)
        position = lax.broadcasted_iota(jnp.int32, (rows, 1), 0) + grp * rows
        match = jnp.sum(jnp.where(position == wanted, inner, 0.0), axis=0, keepdims=True)
        total = jnp.sum(jnp.exp(inner), axis=0, keepdims=True) + jnp.concatenate(
            [queue_sums[g] for g in range(n_grp)], axis=1
        )
        match_sum = match[:, :rows]
        for g in range(1, n_grp):
            match_sum = match_sum + match[:, g * rows : (g + 1) * rows]
        totals[own] = jnp.concatenate([total, match_sum], axis=1)
        matches[grp] = match

    @pl.when(grp == 0)
    def _():
        partner_sums()
        finish_totals()

    pl.when(grp > 0)(finish_totals)

    pl.semaphore_wait(core_sem, 1)

    def total_copy(device):
        remote(totals.at[own], totals.at[own], total_send, total_recv, device).start()

    def to_row(i):
        row = i + (i >= me).astype(jnp.int32)
        each(n_grp, lambda g: total_copy((row, lax.rem(grp + g, n_grp))))

    each(n_dp - 1, to_row)
    each(n_grp - 1, lambda k: total_copy(group_member(k)))
    each(
        n_grp - 1,
        lambda k: remote(
            matches.at[grp], matches.at[grp], match_send, match_recv, group_member(k)
        ).start(),
    )

    if n_chips > 1:
        whole(stat_send, relay_recv, stats.at[0], n_chips - 1).wait_send()

    @pl.when(last)
    def _():
        whole(relay_send, relay_recv, stats.at[0], 1).wait_send()
        if direct > 1:
            whole(stat_send, relay_recv, stats.at[0], direct - 1).wait_send()

    @pl.when(jnp.logical_not(last))
    def _():
        whole(relay_send, relay_recv, stats.at[0], n_chips).wait_send()
        if direct > 0:
            whole(stat_send, relay_recv, stats.at[0], direct).wait_send()

    if n_grp > 1:
        remote(others, others, pos_send, pos_recv, neighbour).wait_send()
        whole(query_send, query_recv.at[0], group_queries, n_grp - 1).wait_send()
        whole(match_send, match_recv, matches, n_grp - 1).wait_recv()
        whole(match_send, match_recv, matches, n_grp - 1).wait_send()
    whole(total_send, total_recv, totals, n_all - 1).wait_send()
    whole(total_send, total_recv, totals, n_all - 1).wait_recv()

    span = pl.ds(pl.multiple_of(grp * rows, rows), rows)
    own_total = totals[me, :, span]
    own_match = matches[0, :, span]
    gathered = totals[pl.ds(0, n_dp)]
    for g in range(1, n_grp):
        own_total = own_total + totals[g * n_dp + me, :, span]
        own_match = own_match + matches[g, :, span]
        gathered = gathered + totals[pl.ds(g * n_dp, n_dp)]
    result[pl.ds(0, 1), :] = jnp.log(own_total) - own_match
    gathered = gathered.reshape(n_dp, columns + rows)
    logs = jnp.sum(jnp.log(gathered[:, :columns]), axis=0, keepdims=True)
    found = jnp.sum(gathered[:, columns:], axis=0, keepdims=True)
    mean = (jnp.sum(logs, axis=1, keepdims=True) - jnp.sum(found, axis=1, keepdims=True)) / (
        rows * n_all
    )
    result[pl.ds(1, 1), :] = jnp.broadcast_to(mean, (1, rows))


def finish(result, losses, mean_loss):
    losses[...] = result[pl.ds(0, 1), :]
    mean_loss[...] = result[pl.ds(1, 1), pl.ds(0, 1)]


def body(
    n_dp,
    n_grp,
    key_inputs,
    query_inputs,
    key_weight,
    query_weight,
    queue,
    shuffle_masks,
    write_pointer,
    positives,
):
    rows, d_in = key_inputs.shape
    width = key_weight.shape[1]
    subs = shuffle_masks.shape[0]
    columns = rows * n_grp
    dma = pltpu.SemaphoreType.DMA
    vector = pl.BlockSpec(memory_space=pltpu.VMEM)
    result = pl.pallas_call(
        functools.partial(kernel, n_dp, n_grp),
        out_shape=pltpu.VMEM((2, rows), jnp.float32),
        in_specs=[pl.BlockSpec(memory_space=pltpu.HBM)] * 8,
        out_specs=vector,
        scratch_shapes=[
            pltpu.VMEM((rows, d_in), jnp.bfloat16),
            pltpu.VMEM((d_in, width), jnp.bfloat16),
            pltpu.VMEM((rows, d_in), jnp.bfloat16),
            pltpu.VMEM((d_in, width), jnp.bfloat16),
            pltpu.VMEM(queue.shape, jnp.bfloat16),
            pltpu.VMEM((rows, width), jnp.float32),
            pltpu.VMEM((2, n_dp // 2, 2 * subs, width), jnp.bfloat16),
            pltpu.VMEM((n_dp, subs, width), jnp.float32),
            pltpu.VMEM((n_dp, subs, width), jnp.float32),
            pltpu.VMEM((n_grp, rows, width), jnp.bfloat16),
            pltpu.VMEM((n_grp, 1, rows), jnp.int32),
            pltpu.VMEM((n_grp, 1, rows), jnp.float32),
            pltpu.VMEM((n_grp * n_dp, 1, columns + rows), jnp.float32),
            pltpu.VMEM((n_grp, 1, columns), jnp.float32),
            pltpu.SMEM((subs,), jnp.int32),
            pltpu.SMEM((1,), jnp.int32),
            dma((4 * CHUNKS + 4,)),
            dma,
            dma,
            dma,
            dma,
            dma,
            dma((n_grp,)),
            dma,
            dma,
            dma,
            dma,
            dma,
            dma,
            pltpu.SemaphoreType.REGULAR,
            pltpu.SemaphoreType.REGULAR,
        ],
        compiler_params=pltpu.CompilerParams(
            collective_id=0, has_side_effects=True, vmem_limit_bytes=56 * 2**20
        ),
        name="contrast",
    )(
        key_inputs,
        query_inputs,
        key_weight,
        query_weight,
        queue,
        shuffle_masks,
        write_pointer,
        positives.reshape(1, rows),
    )
    losses, mean_loss = pl.pallas_call(
        finish,
        out_shape=(
            jax.ShapeDtypeStruct((1, rows), jnp.float32),
            jax.ShapeDtypeStruct((1, 1), jnp.float32),
        ),
        in_specs=[vector],
        out_specs=(vector, vector),
        compiler_params=pltpu.CompilerParams(vmem_limit_bytes=2**20),
        name="finish",
    )(result)
    return losses.reshape(rows), mean_loss.reshape(1)


def solution(mesh):
    placed = (
        P(("dp", "grp"), None),
        P(("dp", "grp"), None),
        P(),
        P(),
        P("grp", None),
        P(),
        P(),
        P(("dp", "grp")),
    )
    return jax.shard_map(
        functools.partial(body, mesh.shape["dp"], mesh.shape["grp"]),
        mesh=mesh,
        in_specs=placed,
        out_specs=(P(("dp", "grp")), P()),
        check_vma=False,
    )
```
